32 devices in a mesh: seq: 8 (over z, core), fsdp: 4 (over y, x).
Axes of the slice: x: 2, y: 2, z: 4, core: 2. Of those that a mesh axis runs over, the one named last changes fastest.
Arguments:
- layer_inputs: bfloat16 [4, 1024, 4096], P('fsdp', 'seq'), may hold values from -8 to 8
- queries: bfloat16 [4, 1024, 4096], P('fsdp', 'seq'), may hold values from -6 to 6
- key_states: bfloat16 [4, 1024, 512], P('fsdp', 'seq'), may hold values from -4 to 4
- value_states: bfloat16 [4, 1024, 512], P('fsdp', 'seq'), may hold values from -1.75 to 1.75
- output_gradient: bfloat16 [4, 1024, 4096], P('fsdp', 'seq'), may hold values from -1.75 to 1.75
- doc_blocks: int32 [4, 4], P('fsdp'), may hold values from 1 to 3, 8 in all within a row
Outputs:
- query_grad: bfloat16 [4, 1024, 4096], P('fsdp', 'seq')
- key_grad: bfloat16 [4, 1024, 512], P('fsdp', 'seq')
- value_grad: bfloat16 [4, 1024, 512], P('fsdp', 'seq')
- value_weight_grad: bfloat16 [4096, 512], P('fsdp')
The draws below stay inside these ranges and needn't reach their ends.
Inputs may be any that keep to these rules, and one draw needn't show every extreme that they name: `doc_blocks`: the lengths of each packed row sum to 8, and each row has a document of exactly 3 blocks.
All inputs are finite; a program needn't handle non-finite values.
Results may differ from the reference program's by a relative error of at most 0.017.
Values may be sent and summed in bfloat16 or wider, within the bound.
A program may use at most 64 MiB of HBM per device.

```python
import math
import jax
import jax.numpy as jnp
import numpy as np
from jax import lax

MODEL_WIDTH = 4096
HQ = 32
KEY_VALUE_HEADS = 4
HEAD_SIZE = 128
ROWS_DEV = 128
BLOCK = 128
MOST = 3
QUERY_PER_KEY = 8
QUERY_WIDTH = 4096
KVW = 512
PACKED_ROWS = 4
PACKED_LENGTH = 1024
NBLK = 8
NDOCS = 4
BACK = 2
KEYS = 384
N_SEQ = 8


def paired_draw(key):
    base_key = jax.random.fold_in(key, 4099)
    key_q, key_k = jax.random.split(base_key, 2)
    query_vals = jnp.clip(jax.random.normal(key_q, (PACKED_ROWS, PACKED_LENGTH, QUERY_WIDTH), jnp.float32), -4.0, 4.0)
    key_vals = jnp.clip(jax.random.normal(key_k, (PACKED_ROWS, PACKED_LENGTH, KVW), jnp.float32), -4.0, 4.0)
    return (query_vals, key_vals)


def draw_queries(key, part):
    return paired_draw(key)[0].astype(jnp.bfloat16)


def draw_key_states(key, part):
    return paired_draw(key)[1].astype(jnp.bfloat16)


def raised(entries, key, source, target, shards_of, factor):
    def block_of(position):
        return (jnp.arange(entries.shape[position]) // (entries.shape[position] // shards_of)).reshape((-1,) + (1,) * (entries.ndim - 1 - position))

    near = jax.random.permutation(key, shards_of)[block_of(target)]
    other_side = (block_of(target) + shards_of // 2) % shards_of
    return jnp.where((block_of(source) == near) | (block_of(source) == other_side), factor * entries, entries)


def block_levels(key, dims, shards, low, largest):
    def one(position, shards_of):
        steps = jax.random.uniform(jax.random.fold_in(jax.random.fold_in(key, 6), position), (shards_of,), jnp.float32, low / len(shards), largest / len(shards))
        return jnp.repeat(jnp.exp(steps), dims[position] // shards_of).reshape((-1,) + (1,) * (len(dims) - position - 1))

    level = one(*shards[0])
    for cut in shards[1:]:
        level = level * one(*cut)
    return level


def length_profile(count, total, most, skew):
    loads = [(1 << 20) // math.isqrt(standing ** skew) + 1 for standing in range(2, count + 1)]
    rest, counts = total - most - (count - 1), [1] * (count - 1)
    while rest > 0:
        movable = [i for i in range(count - 1) if counts[i] < most]
        pool, budget = sum([loads[i] for i in movable]), rest
        for i in movable:
            addition = min(most - counts[i], max(1, budget * loads[i] // pool), rest)
            counts[i] = counts[i] + addition
            rest = rest - addition
    return np.array([most] + counts)


def ragged_sizes(stream_key, count, total, bound, slope):
    if count == 2:
        one = jax.random.randint(stream_key, (), max(1, total - bound), min(bound, total - 1) + 1)
        return jnp.stack([one, total - one])
    sizes = jnp.asarray(length_profile(count, total, bound, slope), jnp.int32)
    couples = (count - 1) // 2
    giver, receiver = sizes[1:1 + 2 * couples:2], sizes[2:2 + 2 * couples:2]
    margin = jnp.minimum(giver - 1, bound - receiver)
    passed = jax.random.randint(jax.random.fold_in(stream_key, 1), (couples,), 0, 1 << 20) % (margin + 1)
    sizes = sizes.at[1:1 + 2 * couples:2].set(giver - passed).at[2:2 + 2 * couples:2].set(receiver + passed)
    return sizes[jax.random.permutation(jax.random.fold_in(stream_key, 2), count)]


def scatter_about(key, shape, width, most, cuts=(), kind=jnp.bfloat16):
    loudness = block_levels(key, shape, cuts, -0.22, 0.18) if cuts else 1.0
    drawn = jax.random.normal(key, shape, jnp.float32) * width * loudness
    return jnp.minimum(jnp.maximum(drawn, -most), most).astype(kind)


def gaussian_with(key, extent, spread, limit, shards, heavy, kind=jnp.bfloat16):
    values = spread * jax.random.normal(key, extent, jnp.float32)
    if shards:
        values = values * block_levels(key, extent, shards, -0.22, 0.18)
    return jnp.clip(raised(values, jax.random.fold_in(key, 3), *heavy), -limit, limit).astype(kind)


def setup_inputs(seed: int = 0) -> dict:
    splits = jax.random.split(jax.random.key(seed), 7)
    layer_inputs = gaussian_with(splits[0], (PACKED_ROWS, PACKED_LENGTH, MODEL_WIDTH), 1.0, 8.0, ((0, 4), (1, 8)), (0, 2, 4, 2.0))
    queries = draw_queries(jax.random.fold_in(splits[6], 71), 0)
    key_states = draw_key_states(jax.random.fold_in(splits[6], 71), 0)
    value_states = scatter_about(splits[3], (PACKED_ROWS, PACKED_LENGTH, KVW), 0.3, 1.75, ((0, 4), (1, 8)))
    output_gradient = scatter_about(splits[4], (PACKED_ROWS, PACKED_LENGTH, QUERY_WIDTH), 0.3, 1.75, ((0, 4), (1, 8)))
    doc_blocks = jax.vmap(lambda own: ragged_sizes(own, NDOCS, NBLK, MOST, 2))(jax.random.split(splits[5], PACKED_ROWS)).reshape((PACKED_ROWS, NDOCS)).astype(jnp.int32)
    return {"layer_inputs": layer_inputs, "queries": queries, "key_states": key_states, "value_states": value_states, "output_gradient": output_gradient, "doc_blocks": doc_blocks}


def document_ids(positions, doc_ends):
    block_ids = jnp.floor_divide(positions, BLOCK)
    return lax.optimization_barrier(jnp.sum((block_ids[:, None] >= doc_ends[None, :]).astype(jnp.int32), axis=1))

def rounded(values_in):
    return lax.optimization_barrier(values_in.astype(jnp.bfloat16)).astype(jnp.float32)

def window_grads(query_block, gradient_block, window_keys, window_values, first_query, first_key, doc_ends):
    softmax_factor_scale = 1.0 / math.sqrt(HEAD_SIZE)
    token_rows = query_block.shape[0]
    key_number = window_keys.shape[0]
    q_pos = first_query + jnp.arange(token_rows, dtype=jnp.int32)
    k_pos = first_key + jnp.arange(key_number, dtype=jnp.int32)
    same_doc = document_ids(k_pos, doc_ends)[None, :] == document_ids(q_pos, doc_ends)[:, None]
    visible = same_doc & (k_pos[None, :] >= 0) & (k_pos[None, :] <= q_pos[:, None])
    query_head_states = query_block.astype(jnp.float32).reshape(token_rows, KEY_VALUE_HEADS, QUERY_PER_KEY, HEAD_SIZE)
    gradient_heads = gradient_block.astype(jnp.float32).reshape(token_rows, KEY_VALUE_HEADS, QUERY_PER_KEY, HEAD_SIZE)
    key_head_states = window_keys.astype(jnp.float32).reshape(key_number, KEY_VALUE_HEADS, HEAD_SIZE)
    value_head_states = window_values.astype(jnp.float32).reshape(key_number, KEY_VALUE_HEADS, HEAD_SIZE)
    scores = jnp.einsum('rghd,kgd->ghrk', query_head_states, key_head_states) * softmax_factor_scale
    scores = jnp.where(visible[None, None], scores, -jnp.inf)
    row_max = lax.optimization_barrier(jnp.max(scores, axis=-1, keepdims=True))
    exps = jnp.exp(scores - row_max)
    probs = exps / lax.optimization_barrier(jnp.sum(exps, axis=-1, keepdims=True))
    d_probs = jnp.einsum('rghd,kgd->ghrk', gradient_heads, value_head_states)
    deltas = lax.optimization_barrier(jnp.sum(probs * d_probs, axis=-1, keepdims=True))
    score_gradient = rounded(probs * (d_probs - deltas))
    probability_reduced = rounded(probs)
    value_portion = jnp.einsum('eozf,zeol->fel', probability_reduced, gradient_heads).reshape(key_number, KEY_VALUE_HEADS * HEAD_SIZE)
    key_portion = (jnp.einsum('eozf,zeol->fel', score_gradient, query_head_states) * softmax_factor_scale).reshape(key_number, KEY_VALUE_HEADS * HEAD_SIZE)
    query_portion = jnp.einsum('ghrk,kgd->rghd', score_gradient, key_head_states) * softmax_factor_scale
    return (query_portion.reshape(token_rows, KEY_VALUE_HEADS * QUERY_PER_KEY * HEAD_SIZE).astype(jnp.bfloat16), key_portion, value_portion)

def reference(layer_inputs, queries, key_states, value_states, output_gradient, doc_blocks):
    pad_rows = BACK * ROWS_DEV
    key_value_width = KEY_VALUE_HEADS * HEAD_SIZE

    def one_pack(weight_total, pack_data):
        inputs_p, queries_p, keys_p, values_p, grads_p, lengths_p = pack_data
        doc_ends = jnp.cumsum(lengths_p).astype(jnp.int32)
        zero_rows = jnp.zeros((pad_rows, key_value_width), keys_p.dtype)
        keys_pad = jnp.concatenate([zero_rows, keys_p], axis=0)
        values_pad = jnp.concatenate([zero_rows, values_p], axis=0)

        def one_shard(sums, shard_no):
            key_sum, value_sum = sums
            first_row = (shard_no * ROWS_DEV).astype(jnp.int32)
            query_block = lax.dynamic_slice_in_dim(queries_p, first_row, ROWS_DEV, 0)
            gradient_block = lax.dynamic_slice_in_dim(grads_p, first_row, ROWS_DEV, 0)
            window_keys = lax.dynamic_slice_in_dim(keys_pad, first_row, KEYS, 0)
            window_values = lax.dynamic_slice_in_dim(values_pad, first_row, KEYS, 0)
            query_portion, key_portion, value_portion = window_grads(query_block, gradient_block, window_keys, window_values, first_row, first_row - pad_rows, doc_ends)
            key_sum = lax.dynamic_update_slice_in_dim(key_sum, lax.dynamic_slice_in_dim(key_sum, first_row, KEYS, 0) + key_portion, first_row, 0)
            value_sum = lax.dynamic_update_slice_in_dim(value_sum, lax.dynamic_slice_in_dim(value_sum, first_row, KEYS, 0) + value_portion, first_row, 0)
            return ((key_sum, value_sum), query_portion)
        empty_sum = jnp.zeros((PACKED_LENGTH + pad_rows, key_value_width), jnp.float32)
        (key_sum, value_sum), query_blocks = lax.scan(one_shard, (empty_sum, empty_sum), jnp.arange(N_SEQ, dtype=jnp.int32))
        key_grad = key_sum[pad_rows:].astype(jnp.bfloat16)
        value_grad = value_sum[pad_rows:].astype(jnp.bfloat16)
        query_grad = query_blocks.reshape(PACKED_LENGTH, HQ * HEAD_SIZE)

        def one_run(total, run_pair):
            run_inputs, run_values = run_pair
            partial_w = jnp.dot(run_inputs.T, run_values, preferred_element_type=jnp.float32)
            return (total + rounded(partial_w), None)
        weight_total, _ = lax.scan(one_run, weight_total, (inputs_p.reshape(N_SEQ, ROWS_DEV, MODEL_WIDTH), value_grad.reshape(N_SEQ, ROWS_DEV, key_value_width)))
        return (weight_total, (query_grad, key_grad, value_grad))
    weight_initial = jnp.zeros((MODEL_WIDTH, KEY_VALUE_HEADS * HEAD_SIZE), jnp.float32)
    weight_total, outs_all = lax.scan(one_pack, weight_initial, (layer_inputs, queries, key_states, value_states, output_gradient, doc_blocks))
    query_grad, key_grad, value_grad = outs_all
    value_weight_grad = (weight_total / math.sqrt(PACKED_ROWS * PACKED_LENGTH)).astype(jnp.bfloat16)
    return (query_grad, key_grad, value_grad, value_weight_grad)
```

```python
import functools
import math

import jax
import jax.numpy as jnp
from jax import lax
from jax.experimental import pallas as pl
from jax.experimental.pallas import tpu as pltpu
from jax.sharding import PartitionSpec as P

HEAD_SIZE = 128
BLOCK = 128
BACK = 2
PAIR = 2
HALVES = 2
SUB = 4
MESH = pl.DeviceIdType.MESH
F32 = jnp.float32
BF16 = jnp.bfloat16


def matmul(a, b, ca, cb):
    return lax.dot_general(a, b, (((ca,), (cb,)), ((), ())), preferred_element_type=F32)


def kernel(
    n_s, n_f, groups, heads,
    doc_ref, x_hbm, q_hbm, k_hbm, v_hbm, g_hbm,
    dq_out, dk_out, vg_out, w_out,
    q, g, kwin, vwin, xg, probs, bias, dq,
    dv_own, dv_send, dv_recv, dk_own, dk_send, dk_recv, dkb, vgb,
    w_own, pair_send, pair_recv, right_send, left_recv, left_send, right_recv, wfin,
    loc_sem, out_sem, k_ss, k_rs, v_ss, v_rs, x_ss, x_rs,
    dv_ss, dv_rs, dk_ss, dk_rs, vg_ss, vg_rs, p_ss, p_rs,
    r_ss, r_rs, l_ss, l_rs, f_ss, f_rs,
):
    s = lax.axis_index("seq")
    f = lax.axis_index("fsdp")
    rows = q.shape[0]
    width = xg.shape[2]
    kvw = groups * HEAD_SIZE
    keys = (BACK + 1) * rows
    chunks = HALVES * SUB
    half_cols = kvw // HALVES
    half_rows = width // 2
    sub_rows = half_rows // SUB
    core = s % 2
    z = s // 2
    depth = n_s // 2
    sibling = s + 1 - 2 * core
    scale = 1.0 / math.sqrt(HEAD_SIZE)

    def remote(src, dst, ss, rs, to_s, to_f):
        return pltpu.make_async_remote_copy(
            src_ref=src, dst_ref=dst, send_sem=ss, recv_sem=rs,
            device_id={"seq": to_s, "fsdp": to_f}, device_id_type=MESH,
        )

    local = [
        pltpu.make_async_copy(q_hbm.at[0], q, loc_sem.at[0]),
        pltpu.make_async_copy(g_hbm.at[0], g, loc_sem.at[1]),
        pltpu.make_async_copy(k_hbm.at[0], kwin.at[BACK], loc_sem.at[2]),
        pltpu.make_async_copy(v_hbm.at[0], vwin.at[BACK], loc_sem.at[3]),
        pltpu.make_async_copy(
            x_hbm.at[0, :, pl.ds(pl.multiple_of(f * width, 128), width)], xg.at[f], loc_sem.at[4]
        ),
    ]
    for copy in local:
        copy.start()

    barrier = pltpu.get_barrier_semaphore()
    for d in range(1, BACK + 1):
        @pl.when(s >= d)
        def _():
            pl.semaphore_signal(
                barrier, inc=1, device_id={"seq": s - d, "fsdp": f}, device_id_type=MESH
            )

        @pl.when(s + d < n_s)
        def _():
            pl.semaphore_signal(
                barrier, inc=1, device_id={"seq": s + d, "fsdp": f}, device_id_type=MESH
            )
    for j in range(1, n_f):
        pl.semaphore_signal(
            barrier, inc=1, device_id={"seq": s, "fsdp": (f + j) % n_f}, device_id_type=MESH
        )

    def doc_of(block):
        end = jnp.int32(0)
        doc = jnp.int32(0)
        for i in range(doc_ref.shape[1]):
            end = end + doc_ref[0, i]
            doc = doc + jnp.where(block >= end, 1, 0)
        return doc

    mine = doc_of(s)
    for d in range(1, BACK + 1):
        seen = jnp.logical_and(doc_of(s - d) == mine, s >= d)
        level = jnp.where(seen, 0.0, -jnp.inf).astype(F32)
        bias[(BACK - d) * rows : (BACK - d + 1) * rows, :] = jnp.full(
            (rows, PAIR * rows), level, F32
        )
    key_at = lax.broadcasted_iota(jnp.int32, (rows, PAIR * rows), 0)
    query_at = lax.broadcasted_iota(jnp.int32, (rows, PAIR * rows), 1) % rows
    bias[BACK * rows :, :] = jnp.where(key_at <= query_at, 0.0, -jnp.inf).astype(F32)

    for d in range(1, BACK + 1):
        @pl.when(s < d)
        def _():
            kwin[BACK - d] = jnp.zeros((rows, kvw), BF16)
            vwin[BACK - d] = jnp.zeros((rows, kvw), BF16)

        @pl.when(s + d >= n_s)
        def _():
            dv_recv[d - 1] = jnp.zeros((rows, kvw), BF16)
            dk_recv[d - 1] = jnp.zeros((rows, kvw), BF16)

    @pl.when(z == 0)
    def _():
        left_recv[...] = jnp.zeros_like(left_recv)

    @pl.when(z == depth - 1)
    def _():
        right_recv[...] = jnp.zeros_like(right_recv)

    one = lambda c: jnp.where(c, 1, 0)
    pl.semaphore_wait(
        barrier, n_f - 1 + one(s >= 1) + one(s >= 2) + one(s + 1 < n_s) + one(s + 2 < n_s)
    )

    def group_cols(i):
        return pl.ds(pl.multiple_of(i * HEAD_SIZE, HEAD_SIZE), HEAD_SIZE)

    def k_copy(d, i):
        return remote(
            k_hbm.at[0, :, group_cols(i)], kwin.at[BACK - d, :, group_cols(i)],
            k_ss.at[d - 1, i], k_rs.at[d - 1, i], s + d, f,
        )

    def v_copy(d):
        return remote(
            v_hbm.at[0], vwin.at[BACK - d], v_ss.at[d - 1], v_rs.at[d - 1], s + d, f
        )

    def x_copy(j):
        to = (f + j) % n_f
        return remote(
            x_hbm.at[0, :, pl.ds(pl.multiple_of(to * width, 128), width)], xg.at[f],
            x_ss.at[j], x_rs.at[j], s, to,
        )

    for i in range(groups):
        for d in range(1, BACK + 1):
            @pl.when(s + d < n_s)
            def _():
                k_copy(d, i).start()
    for d in range(1, BACK + 1):
        @pl.when(s + d < n_s)
        def _():
            v_copy(d).start()
    for j in range(1, n_f):
        x_copy(j).start()

    for copy in local[:3]:
        copy.wait()

    def back_copy(send, recv, ss, rs, d, i):
        return remote(
            send.at[d - 1, :, group_cols(i)], recv.at[d - 1, :, group_cols(i)],
            ss.at[d - 1, i], rs.at[d - 1, i], s - d, f,
        )

    def pair_of(ref, i, j):
        first = (i * heads + j * PAIR) * HEAD_SIZE
        return jnp.concatenate(
            [
                ref[:, pl.ds(pl.multiple_of(first + n * HEAD_SIZE, HEAD_SIZE), HEAD_SIZE)]
                for n in range(PAIR)
            ],
            axis=0,
        )

    def give_back(total, own, send, recv, ss, rs, i):
        own[:, group_cols(i)] = total[BACK * rows :]
        for d in range(1, BACK + 1):
            send[d - 1, :, group_cols(i)] = total[(BACK - d) * rows : (BACK - d + 1) * rows].astype(
                BF16
            )

            @pl.when(s >= d)
            def _():
                back_copy(send, recv, ss, rs, d, i).start()

    def first_pass(i, carry):
        for d in range(1, BACK + 1):
            @pl.when(s >= d)
            def _():
                k_copy(d, i).wait_recv()
        k_group = kwin[:, :, group_cols(i)].reshape(keys, HEAD_SIZE)
        total = jnp.zeros((keys, HEAD_SIZE), F32)
        for j in range(heads // PAIR):
            scores = matmul(k_group, pair_of(q, i, j), 1, 1)
            scores = scores * (scale * math.log2(math.e)) + bias[...]
            exps = jnp.exp2(scores - jnp.max(scores, axis=0, keepdims=True))
            p = exps * (1.0 / jnp.sum(exps, axis=0, keepdims=True))
            probs[i, j] = p
            total = total + matmul(p.astype(BF16), pair_of(g, i, j), 1, 0)
        give_back(total, dv_own, dv_send, dv_recv, dv_ss, dv_rs, i)
        return carry

    lax.fori_loop(0, groups, first_pass, 0)

    local[3].wait()
    for d in range(1, BACK + 1):
        @pl.when(s >= d)
        def _():
            v_copy(d).wait_recv()

    def second_pass(i, carry):
        k_group = kwin[:, :, group_cols(i)].reshape(keys, HEAD_SIZE)
        v_group = vwin[:, :, group_cols(i)].reshape(keys, HEAD_SIZE)
        k_turned = k_group.T
        total = jnp.zeros((keys, HEAD_SIZE), F32)
        for j in range(heads // PAIR):
            p = probs[i, j]
            d_probs = matmul(v_group, pair_of(g, i, j), 1, 1)
            deltas = jnp.sum(p * d_probs, axis=0, keepdims=True)
            d_scores = (p * (d_probs - deltas)).astype(BF16)
            total = total + matmul(d_scores, pair_of(q, i, j), 1, 0)
            turned = (matmul(k_turned, d_scores, 1, 0) * scale).T.astype(BF16)
            first = (i * heads + j * PAIR) * HEAD_SIZE
            for n in range(PAIR):
                cols = pl.ds(pl.multiple_of(first + n * HEAD_SIZE, HEAD_SIZE), HEAD_SIZE)
                dq[:, cols] = turned[n * rows : (n + 1) * rows]
        give_back(total * scale, dk_own, dk_send, dk_recv, dk_ss, dk_rs, i)
        return carry

    def vg_copy(h, j):
        cols = pl.ds(h * half_cols, half_cols)
        return remote(
            vgb.at[f, :, cols], vgb.at[f, :, cols], vg_ss.at[h, j], vg_rs.at[h, j],
            s, (f + j) % n_f,
        )

    per_half = groups // HALVES

    def collect(own, recv, send, ss, rs, lo, count):
        for i in range(lo, lo + count):
            for d in range(1, BACK + 1):
                @pl.when(s + d < n_s)
                def _():
                    back_copy(send, recv, ss, rs, d, i).wait_recv()
        cols = slice(lo * HEAD_SIZE, (lo + count) * HEAD_SIZE)
        total = own[:, cols]
        for d in range(1, BACK + 1):
            total = total + recv[d - 1, :, cols].astype(F32)
        return total.astype(BF16)

    def value_half(h):
        cols = slice(h * half_cols, (h + 1) * half_cols)
        vgb[f, :, cols] = collect(dv_own, dv_recv, dv_send, dv_ss, dv_rs, h * per_half, per_half)
        for j in range(1, n_f):
            vg_copy(h, j).start()

    def pair_copy(h):
        return remote(
            pair_send.at[h], pair_recv.at[h], p_ss.at[h], p_rs.at[h], sibling, f
        )

    def weight_half(h):
        for j in range(1, n_f):
            vg_copy(h, j).wait_recv()
        values = vgb[:, :, h * half_cols : (h + 1) * half_cols].reshape(n_f * rows, half_cols)

        def part(which):
            lhs = xg[:, :, pl.ds(pl.multiple_of(which * half_rows, half_rows), half_rows)]
            return matmul(lhs.reshape(n_f * rows, half_rows), values, 0, 0)

        pair_send[h] = part(1 - core).astype(BF16)
        pair_copy(h).start()
        w_own[h] = part(core)

    lax.fori_loop(0, 1, second_pass, 0)
    value_half(0)
    lax.fori_loop(1, 3, second_pass, 0) if groups > 3 else None
    value_half(1)
    lax.fori_loop(3 if groups > 3 else 1, groups, second_pass, 0)
    dq_copy = pltpu.make_async_copy(dq, dq_out.at[0], out_sem.at[0])
    dq_copy.start()
    vg_save = pltpu.make_async_copy(vgb.at[f], vg_out.at[0], out_sem.at[1])
    vg_save.start()
    local[4].wait()
    for j in range(1, n_f):
        x_copy(j).wait_recv()
    for h in range(HALVES):
        weight_half(h)
    for h in range(HALVES):
        pair_copy(h).wait_recv()
        w_own[h] = w_own[h] + pair_recv[h].astype(F32)

    def right_copy(c):
        return remote(right_send.at[c], left_recv.at[c], r_ss.at[c], r_rs.at[c], s + 2, f)

    def left_copy(c):
        return remote(left_send.at[c], right_recv.at[c], l_ss.at[c], l_rs.at[c], s - 2, f)

    def place(c, side):
        at = side * half_rows + (c % SUB) * sub_rows
        return wfin.at[
            pl.ds(pl.multiple_of(at, sub_rows), sub_rows),
            pl.ds(pl.multiple_of((c // SUB) * half_cols, half_cols), half_cols),
        ]

    def final_copy(c):
        return remote(place(c, core), place(c, core), f_ss.at[c], f_rs.at[c], sibling, f)

    def own_chunk(c):
        return w_own[c // SUB, pl.ds(pl.multiple_of((c % SUB) * sub_rows, sub_rows), sub_rows), :]

    token_count = n_f * n_s * rows

    def step(t, carry):
        to_right = t - z
        to_left = t - (depth - 1 - z)
        done = t - jnp.maximum(z, depth - 1 - z)

        def inside(c):
            return jnp.logical_and(c >= 0, c < chunks)

        @pl.when(jnp.logical_and(inside(to_right), z > 0))
        def _():
            right_copy(to_right).wait_recv()

        @pl.when(jnp.logical_and(inside(to_right), z < depth - 1))
        def _():
            right_send[to_right] = (own_chunk(to_right) + left_recv[to_right].astype(F32)).astype(
                BF16
            )
            right_copy(to_right).start()

        @pl.when(jnp.logical_and(inside(to_left), z < depth - 1))
        def _():
            left_copy(to_left).wait_recv()

        @pl.when(jnp.logical_and(inside(to_left), z > 0))
        def _():
            left_send[to_left] = (own_chunk(to_left) + right_recv[to_left].astype(F32)).astype(BF16)
            left_copy(to_left).start()

        @pl.when(inside(done))
        def _():
            total = own_chunk(done) + left_recv[done].astype(F32) + right_recv[done].astype(F32)
            place(done, core)[...] = (total * (1.0 / math.sqrt(token_count))).astype(BF16)
            final_copy(done).start()

        return carry

    lax.fori_loop(0, chunks + depth - 1, step, 0)

    dkb[...] = collect(dk_own, dk_recv, dk_send, dk_ss, dk_rs, 0, groups)
    dk_save = pltpu.make_async_copy(dkb, dk_out.at[0], out_sem.at[2])
    dk_save.start()

    def settle(c, carry):
        other = remote(place(c, 1 - core), place(c, 1 - core), f_ss.at[c], f_rs.at[c], sibling, f)
        other.wait_recv()
        final_copy(c).wait_send()

        @pl.when(z < depth - 1)
        def _():
            right_copy(c).wait_send()

        @pl.when(z > 0)
        def _():
            left_copy(c).wait_send()

        return carry

    lax.fori_loop(0, chunks, settle, 0)
    w_save = pltpu.make_async_copy(wfin, w_out, out_sem.at[3])
    w_save.start()
    for d in range(1, BACK + 1):
        @pl.when(s + d < n_s)
        def _():
            v_copy(d).wait_send()
            for i in range(groups):
                k_copy(d, i).wait_send()

        @pl.when(s >= d)
        def _():
            for i in range(groups):
                back_copy(dv_send, dv_recv, dv_ss, dv_rs, d, i).wait_send()
                back_copy(dk_send, dk_recv, dk_ss, dk_rs, d, i).wait_send()
    for j in range(1, n_f):
        x_copy(j).wait_send()
        for h in range(HALVES):
            vg_copy(h, j).wait_send()
    for h in range(HALVES):
        pair_copy(h).wait_send()
    dq_copy.wait()
    vg_save.wait()
    dk_save.wait()
    w_save.wait()


def shards(n_s, n_f, layer_inputs, queries, key_states, value_states, output_gradient, doc_blocks):
    rows = queries.shape[1]
    kvw = key_states.shape[2]
    groups = kvw // HEAD_SIZE
    heads = queries.shape[2] // kvw
    width = layer_inputs.shape[2] // n_f
    chunks = HALVES * SUB
    half_cols = kvw // HALVES
    half_rows = width // 2
    sub_rows = half_rows // SUB
    keys = (BACK + 1) * rows
    V = pltpu.VMEM
    D = pltpu.SemaphoreType.DMA
    scratch = [
        V((rows, queries.shape[2]), BF16),
        V((rows, queries.shape[2]), BF16),
        V((BACK + 1, rows, kvw), BF16),
        V((BACK + 1, rows, kvw), BF16),
        V((n_f, rows, width), BF16),
        V((groups, heads // PAIR, keys, PAIR * rows), F32),
        V((keys, PAIR * rows), F32),
        V((rows, queries.shape[2]), BF16),
        V((rows, kvw), F32),
        V((BACK, rows, kvw), BF16),
        V((BACK, rows, kvw), BF16),
        V((rows, kvw), F32),
        V((BACK, rows, kvw), BF16),
        V((BACK, rows, kvw), BF16),
        V((rows, kvw), BF16),
        V((n_f, rows, kvw), BF16),
        V((HALVES, half_rows, half_cols), F32),
        V((HALVES, half_rows, half_cols), BF16),
        V((HALVES, half_rows, half_cols), BF16),
        V((chunks, sub_rows, half_cols), BF16),
        V((chunks, sub_rows, half_cols), BF16),
        V((chunks, sub_rows, half_cols), BF16),
        V((chunks, sub_rows, half_cols), BF16),
        V((width, kvw), BF16),
        D((5,)), D((4,)),
        D((BACK, groups)), D((BACK, groups)), D((BACK,)), D((BACK,)), D((n_f,)), D((n_f,)),
        D((BACK, groups)), D((BACK, groups)), D((BACK, groups)), D((BACK, groups)),
        D((HALVES, n_f)), D((HALVES, n_f)), D((HALVES,)), D((HALVES,)),
        D((chunks,)), D((chunks,)), D((chunks,)), D((chunks,)), D((chunks,)), D((chunks,)),
    ]
    anywhere = pl.BlockSpec(memory_space=pl.ANY)
    out_shape = [
        jax.ShapeDtypeStruct(queries.shape, BF16),
        jax.ShapeDtypeStruct(key_states.shape, BF16),
        jax.ShapeDtypeStruct(key_states.shape, BF16),
        jax.ShapeDtypeStruct((width, kvw), BF16),
    ]
    return tuple(
        pl.pallas_call(
            functools.partial(kernel, n_s, n_f, groups, heads),
            out_shape=out_shape,
            in_specs=[pl.BlockSpec(memory_space=pltpu.SMEM)] + [anywhere] * 5,
            out_specs=[anywhere] * 4,
            scratch_shapes=scratch,
            compiler_params=pltpu.CompilerParams(collective_id=0, has_side_effects=True),
        )(doc_blocks, layer_inputs, queries, key_states, value_states, output_gradient)
    )


def solution(mesh):
    sizes = dict(mesh.shape)
    return jax.shard_map(
        functools.partial(shards, sizes["seq"], sizes["fsdp"]),
        mesh=mesh,
        in_specs=(P("fsdp", "seq", None),) * 5 + (P("fsdp", None),),
        out_specs=(P("fsdp", "seq", None),) * 3 + (P("fsdp", None),),
        check_vma=False,
    )
```

```python
import functools
import math

import jax
import jax.numpy as jnp
from jax import lax
from jax.experimental import pallas as pl
from jax.experimental.pallas import tpu as pltpu
from jax.sharding import PartitionSpec as P

HEAD_SIZE = 128
BLOCK = 128
BACK = 2
PAIR = 2
HALVES = 2
SUB = 4
SLACK = 3
MESH = pl.DeviceIdType.MESH
F32 = jnp.float32
BF16 = jnp.bfloat16


def matmul(a, b, ca, cb):
    return lax.dot_general(a, b, (((ca,), (cb,)), ((), ())), preferred_element_type=F32)


def kernel(
    n_s, n_f, groups, heads,
    doc_ref, x_hbm, q_hbm, k_hbm, v_hbm, g_hbm,
    dq_out, dk_out, vg_out, w_out,
    q, g, kwin, vwin, xg, probs, bias, dq,
    dv_own, dv_send, dv_recv, dk_own, dk_send, dk_recv, dkb, vgb,
    w_own, pair_send, pair_recv, right_send, left_recv, left_send, right_recv, wfin,
    loc_sem, out_sem, k_ss, k_rs, v_ss, v_rs, x_ss, x_rs,
    dv_ss, dv_rs, dk_ss, dk_rs, vg_ss, vg_rs, p_ss, p_rs,
    r_ss, r_rs, l_ss, l_rs, f_ss, f_rs,
):
    s = lax.axis_index("seq")
    f = lax.axis_index("fsdp")
    rows = q.shape[0]
    width = xg.shape[2]
    kvw = groups * HEAD_SIZE
    keys = (BACK + 1) * rows
    chunks = HALVES * SUB
    half_cols = kvw // HALVES
    half_rows = width // 2
    sub_rows = half_rows // SUB
    core = s % 2
    z = s // 2
    depth = n_s // 2
    sibling = s + 1 - 2 * core
    scale = 1.0 / math.sqrt(HEAD_SIZE)

    def remote(src, dst, ss, rs, to_s, to_f):
        return pltpu.make_async_remote_copy(
            src_ref=src, dst_ref=dst, send_sem=ss, recv_sem=rs,
            device_id={"seq": to_s, "fsdp": to_f}, device_id_type=MESH,
        )

    local = [
        pltpu.make_async_copy(q_hbm.at[0], q, loc_sem.at[0]),
        pltpu.make_async_copy(g_hbm.at[0], g, loc_sem.at[1]),
        pltpu.make_async_copy(k_hbm.at[0], kwin.at[BACK], loc_sem.at[2]),
        pltpu.make_async_copy(v_hbm.at[0], vwin.at[BACK], loc_sem.at[3]),
        pltpu.make_async_copy(
            x_hbm.at[0, :, pl.ds(pl.multiple_of(f * width, 128), width)], xg.at[f], loc_sem.at[4]
        ),
    ]
    for copy in local:
        copy.start()

    barrier = pltpu.get_barrier_semaphore()
    for d in range(1, BACK + 1):
        @pl.when(s >= d)
        def _():
            pl.semaphore_signal(
                barrier, inc=1, device_id={"seq": s - d, "fsdp": f}, device_id_type=MESH
            )

        @pl.when(s + d < n_s)
        def _():
            pl.semaphore_signal(
                barrier, inc=1, device_id={"seq": s + d, "fsdp": f}, device_id_type=MESH
            )
    for j in range(1, n_f):
        pl.semaphore_signal(
            barrier, inc=1, device_id={"seq": s, "fsdp": (f + j) % n_f}, device_id_type=MESH
        )

    def doc_of(block):
        end = jnp.int32(0)
        doc = jnp.int32(0)
        for i in range(doc_ref.shape[1]):
            end = end + doc_ref[0, i]
            doc = doc + jnp.where(block >= end, 1, 0)
        return doc

    mine = doc_of(s)
    for d in range(1, BACK + 1):
        seen = jnp.logical_and(doc_of(s - d) == mine, s >= d)
        level = jnp.where(seen, 0.0, -jnp.inf).astype(F32)
        bias[(BACK - d) * rows : (BACK - d + 1) * rows, :] = jnp.full(
            (rows, PAIR * rows), level, F32
        )
    key_at = lax.broadcasted_iota(jnp.int32, (rows, PAIR * rows), 0)
    query_at = lax.broadcasted_iota(jnp.int32, (rows, PAIR * rows), 1) % rows
    bias[BACK * rows :, :] = jnp.where(key_at <= query_at, 0.0, -jnp.inf).astype(F32)

    for d in range(1, BACK + 1):
        @pl.when(s < d)
        def _():
            kwin[BACK - d] = jnp.zeros((rows, kvw), BF16)
            vwin[BACK - d] = jnp.zeros((rows, kvw), BF16)

        @pl.when(s + d >= n_s)
        def _():
            dv_recv[d - 1] = jnp.zeros((rows, kvw), BF16)
            dk_recv[d - 1] = jnp.zeros((rows, kvw), BF16)

    @pl.when(z == 0)
    def _():
        left_recv[...] = jnp.zeros_like(left_recv)

    @pl.when(z == depth - 1)
    def _():
        right_recv[...] = jnp.zeros_like(right_recv)

    one = lambda c: jnp.where(c, 1, 0)
    pl.semaphore_wait(
        barrier, n_f - 1 + one(s >= 1) + one(s >= 2) + one(s + 1 < n_s) + one(s + 2 < n_s)
    )

    def group_cols(i):
        return pl.ds(pl.multiple_of(i * HEAD_SIZE, HEAD_SIZE), HEAD_SIZE)

    def k_copy(d, i):
        return remote(
            k_hbm.at[0, :, group_cols(i)], kwin.at[BACK - d, :, group_cols(i)],
            k_ss.at[d - 1, i], k_rs.at[d - 1, i], s + d, f,
        )

    def v_copy(d):
        return remote(
            v_hbm.at[0], vwin.at[BACK - d], v_ss.at[d - 1], v_rs.at[d - 1], s + d, f
        )

    def x_copy(j):
        to = (f + j) % n_f
        return remote(
            x_hbm.at[0, :, pl.ds(pl.multiple_of(to * width, 128), width)], xg.at[f],
            x_ss.at[j], x_rs.at[j], s, to,
        )

    for i in range(groups):
        for d in range(1, BACK + 1):
            @pl.when(s + d < n_s)
            def _():
                k_copy(d, i).start()
    for d in range(1, BACK + 1):
        @pl.when(s + d < n_s)
        def _():
            v_copy(d).start()
    for j in range(1, n_f):
        x_copy(j).start()

    for copy in local[:3]:
        copy.wait()

    def back_copy(send, recv, ss, rs, d, i):
        return remote(
            send.at[d - 1, :, group_cols(i)], recv.at[d - 1, :, group_cols(i)],
            ss.at[d - 1, i], rs.at[d - 1, i], s - d, f,
        )

    def pair_of(ref, i, j):
        first = (i * heads + j * PAIR) * HEAD_SIZE
        return jnp.concatenate(
            [
                ref[:, pl.ds(pl.multiple_of(first + n * HEAD_SIZE, HEAD_SIZE), HEAD_SIZE)]
                for n in range(PAIR)
            ],
            axis=0,
        )

    def give_back(total, own, send, recv, ss, rs, i):
        own[:, group_cols(i)] = total[BACK * rows :]
        for d in range(1, BACK + 1):
            send[d - 1, :, group_cols(i)] = total[(BACK - d) * rows : (BACK - d + 1) * rows].astype(
                BF16
            )

            @pl.when(s >= d)
            def _():
                back_copy(send, recv, ss, rs, d, i).start()

    def first_pass(i, carry):
        for d in range(1, BACK + 1):
            @pl.when(s >= d)
            def _():
                k_copy(d, i).wait_recv()
        k_group = kwin[:, :, group_cols(i)].reshape(keys, HEAD_SIZE)
        total = jnp.zeros((keys, HEAD_SIZE), F32)
        for j in range(heads // PAIR):
            scores = matmul(k_group, pair_of(q, i, j), 1, 1)
            scores = scores * (scale * math.log2(math.e)) + bias[...]
            exps = jnp.exp2(scores - jnp.max(scores, axis=0, keepdims=True))
            p = exps * (1.0 / jnp.sum(exps, axis=0, keepdims=True))
            probs[i, j] = p
            total = total + matmul(p.astype(BF16), pair_of(g, i, j), 1, 0)
        give_back(total, dv_own, dv_send, dv_recv, dv_ss, dv_rs, i)
        return carry

    lax.fori_loop(0, groups, first_pass, 0)

    local[3].wait()
    for d in range(1, BACK + 1):
        @pl.when(s >= d)
        def _():
            v_copy(d).wait_recv()

    def second_pass(i, carry):
        k_group = kwin[:, :, group_cols(i)].reshape(keys, HEAD_SIZE)
        v_group = vwin[:, :, group_cols(i)].reshape(keys, HEAD_SIZE)
        k_turned = k_group.T
        total = jnp.zeros((keys, HEAD_SIZE), F32)
        for j in range(heads // PAIR):
            p = probs[i, j]
            d_probs = matmul(v_group, pair_of(g, i, j), 1, 1)
            deltas = jnp.sum(p * d_probs, axis=0, keepdims=True)
            d_scores = (p * (d_probs - deltas)).astype(BF16)
            total = total + matmul(d_scores, pair_of(q, i, j), 1, 0)
            turned = (matmul(k_turned, d_scores, 1, 0) * scale).T.astype(BF16)
            first = (i * heads + j * PAIR) * HEAD_SIZE
            for n in range(PAIR):
                cols = pl.ds(pl.multiple_of(first + n * HEAD_SIZE, HEAD_SIZE), HEAD_SIZE)
                dq[:, cols] = turned[n * rows : (n + 1) * rows]
        give_back(total * scale, dk_own, dk_send, dk_recv, dk_ss, dk_rs, i)
        return carry

    def vg_copy(h, j):
        cols = pl.ds(h * half_cols, half_cols)
        return remote(
            vgb.at[f, :, cols], vgb.at[f, :, cols], vg_ss.at[h, j], vg_rs.at[h, j],
            s, (f + j) % n_f,
        )

    per_half = groups // HALVES

    def collect(own, recv, send, ss, rs, lo, count):
        for i in range(lo, lo + count):
            for d in range(1, BACK + 1):
                @pl.when(s + d < n_s)
                def _():
                    back_copy(send, recv, ss, rs, d, i).wait_recv()
        cols = slice(lo * HEAD_SIZE, (lo + count) * HEAD_SIZE)
        total = own[:, cols]
        for d in range(1, BACK + 1):
            total = total + recv[d - 1, :, cols].astype(F32)
        return total.astype(BF16)

    def value_half(h):
        cols = slice(h * half_cols, (h + 1) * half_cols)
        vgb[f, :, cols] = collect(dv_own, dv_recv, dv_send, dv_ss, dv_rs, h * per_half, per_half)
        for j in range(1, n_f):
            vg_copy(h, j).start()

    def pair_copy(h):
        return remote(
            pair_send.at[h], pair_recv.at[h], p_ss.at[h], p_rs.at[h], sibling, f
        )

    def weight_half(h):
        for j in range(1, n_f):
            vg_copy(h, j).wait_recv()
        values = vgb[:, :, h * half_cols : (h + 1) * half_cols].reshape(n_f * rows, half_cols)

        def part(which):
            lhs = xg[:, :, pl.ds(pl.multiple_of(which * half_rows, half_rows), half_rows)]
            return matmul(lhs.reshape(n_f * rows, half_rows), values, 0, 0)

        pair_send[h] = part(1 - core).astype(BF16)
        pair_copy(h).start()
        w_own[h] = part(core)

    lax.fori_loop(0, 1, second_pass, 0)
    value_half(0)
    lax.fori_loop(1, 3, second_pass, 0) if groups > 3 else None
    value_half(1)
    lax.fori_loop(3 if groups > 3 else 1, groups, second_pass, 0)
    dq_copy = pltpu.make_async_copy(dq, dq_out.at[0], out_sem.at[0])
    dq_copy.start()
    vg_save = pltpu.make_async_copy(vgb.at[f], vg_out.at[0], out_sem.at[1])
    vg_save.start()
    local[4].wait()
    for j in range(1, n_f):
        x_copy(j).wait_recv()
    for h in range(HALVES):
        weight_half(h)
    for h in range(HALVES):
        pair_copy(h).wait_recv()
        w_own[h] = w_own[h] + pair_recv[h].astype(F32)

    def right_copy(c):
        return remote(right_send.at[c], left_recv.at[c], r_ss.at[c], r_rs.at[c], s + 2, f)

    def left_copy(c):
        return remote(left_send.at[c], right_recv.at[c], l_ss.at[c], l_rs.at[c], s - 2, f)

    def place(c, side):
        at = side * half_rows + (c % SUB) * sub_rows
        return wfin.at[
            pl.ds(pl.multiple_of(at, sub_rows), sub_rows),
            pl.ds(pl.multiple_of((c // SUB) * half_cols, half_cols), half_cols),
        ]

    def final_copy(c):
        return remote(place(c, core), place(c, core), f_ss.at[c], f_rs.at[c], sibling, f)

    def own_chunk(c):
        return w_own[c // SUB, pl.ds(pl.multiple_of((c % SUB) * sub_rows, sub_rows), sub_rows), :]

    token_count = n_f * n_s * rows

    def step(t, carry):
        to_right = t - SLACK * z
        to_left = t - SLACK * (depth - 1 - z)
        done = t - SLACK * jnp.maximum(z, depth - 1 - z)

        def inside(c):
            return jnp.logical_and(c >= 0, c < chunks)

        @pl.when(jnp.logical_and(inside(to_right), z > 0))
        def _():
            right_copy(to_right).wait_recv()

        @pl.when(jnp.logical_and(inside(to_right), z < depth - 1))
        def _():
            right_send[to_right] = (own_chunk(to_right) + left_recv[to_right].astype(F32)).astype(
                BF16
            )
            right_copy(to_right).start()

        @pl.when(jnp.logical_and(inside(to_left), z < depth - 1))
        def _():
            left_copy(to_left).wait_recv()

        @pl.when(jnp.logical_and(inside(to_left), z > 0))
        def _():
            left_send[to_left] = (own_chunk(to_left) + right_recv[to_left].astype(F32)).astype(BF16)
            left_copy(to_left).start()

        @pl.when(inside(done))
        def _():
            total = own_chunk(done) + left_recv[done].astype(F32) + right_recv[done].astype(F32)
            place(done, core)[...] = (total * (1.0 / math.sqrt(token_count))).astype(BF16)
            final_copy(done).start()

        return carry

    lax.fori_loop(0, chunks + SLACK * (depth - 1), step, 0)

    dkb[...] = collect(dk_own, dk_recv, dk_send, dk_ss, dk_rs, 0, groups)
    dk_save = pltpu.make_async_copy(dkb, dk_out.at[0], out_sem.at[2])
    dk_save.start()

    def settle(c, carry):
        other = remote(place(c, 1 - core), place(c, 1 - core), f_ss.at[c], f_rs.at[c], sibling, f)
        other.wait_recv()
        final_copy(c).wait_send()

        @pl.when(z < depth - 1)
        def _():
            right_copy(c).wait_send()

        @pl.when(z > 0)
        def _():
            left_copy(c).wait_send()

        return carry

    lax.fori_loop(0, chunks, settle, 0)
    w_save = pltpu.make_async_copy(wfin, w_out, out_sem.at[3])
    w_save.start()
    for d in range(1, BACK + 1):
        @pl.when(s + d < n_s)
        def _():
            v_copy(d).wait_send()
            for i in range(groups):
                k_copy(d, i).wait_send()

        @pl.when(s >= d)
        def _():
            for i in range(groups):
                back_copy(dv_send, dv_recv, dv_ss, dv_rs, d, i).wait_send()
                back_copy(dk_send, dk_recv, dk_ss, dk_rs, d, i).wait_send()
    for j in range(1, n_f):
        x_copy(j).wait_send()
        for h in range(HALVES):
            vg_copy(h, j).wait_send()
    for h in range(HALVES):
        pair_copy(h).wait_send()
    dq_copy.wait()
    vg_save.wait()
    dk_save.wait()
    w_save.wait()


def settle_outputs(*refs):
    sources, outs, held = refs[:4], refs[4:8], refs[8:12]
    in_sem, out_sem = refs[12:]
    loads, saves = [], []
    for i in range(4):
        loads.append(pltpu.make_async_copy(sources[i], held[i], in_sem.at[i]))
        saves.append(pltpu.make_async_copy(held[i], outs[i], out_sem.at[i]))
    for load in loads:
        load.start()
    for load, save in zip(loads, saves):
        load.wait()
        save.start()
    for save in saves:
        save.wait()


def shards(n_s, n_f, layer_inputs, queries, key_states, value_states, output_gradient, doc_blocks):
    rows = queries.shape[1]
    kvw = key_states.shape[2]
    groups = kvw // HEAD_SIZE
    heads = queries.shape[2] // kvw
    width = layer_inputs.shape[2] // n_f
    chunks = HALVES * SUB
    half_cols = kvw // HALVES
    half_rows = width // 2
    sub_rows = half_rows // SUB
    keys = (BACK + 1) * rows
    V = pltpu.VMEM
    D = pltpu.SemaphoreType.DMA
    scratch = [
        V((rows, queries.shape[2]), BF16),
        V((rows, queries.shape[2]), BF16),
        V((BACK + 1, rows, kvw), BF16),
        V((BACK + 1, rows, kvw), BF16),
        V((n_f, rows, width), BF16),
        V((groups, heads // PAIR, keys, PAIR * rows), F32),
        V((keys, PAIR * rows), F32),
        V((rows, queries.shape[2]), BF16),
        V((rows, kvw), F32),
        V((BACK, rows, kvw), BF16),
        V((BACK, rows, kvw), BF16),
        V((rows, kvw), F32),
        V((BACK, rows, kvw), BF16),
        V((BACK, rows, kvw), BF16),
        V((rows, kvw), BF16),
        V((n_f, rows, kvw), BF16),
        V((HALVES, half_rows, half_cols), F32),
        V((HALVES, half_rows, half_cols), BF16),
        V((HALVES, half_rows, half_cols), BF16),
        V((chunks, sub_rows, half_cols), BF16),
        V((chunks, sub_rows, half_cols), BF16),
        V((chunks, sub_rows, half_cols), BF16),
        V((chunks, sub_rows, half_cols), BF16),
        V((width, kvw), BF16),
        D((5,)), D((4,)),
        D((BACK, groups)), D((BACK, groups)), D((BACK,)), D((BACK,)), D((n_f,)), D((n_f,)),
        D((BACK, groups)), D((BACK, groups)), D((BACK, groups)), D((BACK, groups)),
        D((HALVES, n_f)), D((HALVES, n_f)), D((HALVES,)), D((HALVES,)),
        D((chunks,)), D((chunks,)), D((chunks,)), D((chunks,)), D((chunks,)), D((chunks,)),
    ]
    anywhere = pl.BlockSpec(memory_space=pl.ANY)
    out_shape = [
        jax.ShapeDtypeStruct(queries.shape, BF16),
        jax.ShapeDtypeStruct(key_states.shape, BF16),
        jax.ShapeDtypeStruct(key_states.shape, BF16),
        jax.ShapeDtypeStruct((width, kvw), BF16),
    ]
    made = (
        pl.pallas_call(
            functools.partial(kernel, n_s, n_f, groups, heads),
            out_shape=out_shape,
            in_specs=[pl.BlockSpec(memory_space=pltpu.SMEM)] + [anywhere] * 5,
            out_specs=[anywhere] * 4,
            scratch_shapes=scratch,
            compiler_params=pltpu.CompilerParams(collective_id=0, has_side_effects=True),
        )(doc_blocks, layer_inputs, queries, key_states, value_states, output_gradient)
    )
    return tuple(
        pl.pallas_call(
            settle_outputs,
            out_shape=out_shape,
            in_specs=[anywhere] * 4,
            out_specs=[anywhere] * 4,
            scratch_shapes=[V(o.shape, BF16) for o in out_shape] + [D((4,)), D((4,))],
        )(*made)
    )


def solution(mesh):
    sizes = dict(mesh.shape)
    return jax.shard_map(
        functools.partial(shards, sizes["seq"], sizes["fsdp"]),
        mesh=mesh,
        in_specs=(P("fsdp", "seq", None),) * 5 + (P("fsdp", None),),
        out_specs=(P("fsdp", "seq", None),) * 3 + (P("fsdp", None),),
        check_vma=False,
    )
```

```python
import functools
import math

import jax
import jax.numpy as jnp
from jax import lax
from jax.experimental import pallas as pl
from jax.experimental.pallas import tpu as pltpu
from jax.sharding import PartitionSpec as P

HEAD_SIZE = 128
BLOCK = 128
BACK = 2
PAIR = 2
HALVES = 2
SUB = 4
SLACK = 3
MESH = pl.DeviceIdType.MESH
F32 = jnp.float32
BF16 = jnp.bfloat16


def matmul(a, b, ca, cb):
    return lax.dot_general(a, b, (((ca,), (cb,)), ((), ())), preferred_element_type=F32)


def kernel(
    n_s, n_f, groups, heads,
    doc_ref, x_hbm, q_hbm, k_hbm, v_hbm, g_hbm,
    dq_out, dk_out, vg_out, w_out,
    q, g, kwin, vwin, xg, probs, bias, dq,
    dv_own, dv_send, dv_recv, dk_own, dk_send, dk_recv, dkb, vgb,
    w_own, pair_send, pair_recv, right_send, left_recv, left_send, right_recv, wfin,
    loc_sem, out_sem, k_ss, k_rs, v_ss, v_rs, x_ss, x_rs,
    dv_ss, dv_rs, dk_ss, dk_rs, vg_ss, vg_rs, p_ss, p_rs,
    r_ss, r_rs, l_ss, l_rs, f_ss, f_rs,
):
    s = lax.axis_index("seq")
    f = lax.axis_index("fsdp")
    rows = q.shape[0]
    width = xg.shape[2]
    kvw = groups * HEAD_SIZE
    keys = (BACK + 1) * rows
    chunks = HALVES * SUB
    half_cols = kvw // HALVES
    half_rows = width // 2
    sub_rows = half_rows // SUB
    core = s % 2
    z = s // 2
    depth = n_s // 2
    sibling = s + 1 - 2 * core
    scale = 1.0 / math.sqrt(HEAD_SIZE)

    def remote(src, dst, ss, rs, to_s, to_f):
        return pltpu.make_async_remote_copy(
            src_ref=src, dst_ref=dst, send_sem=ss, recv_sem=rs,
            device_id={"seq": to_s, "fsdp": to_f}, device_id_type=MESH,
        )

    local = [
        pltpu.make_async_copy(q_hbm.at[0], q, loc_sem.at[0]),
        pltpu.make_async_copy(g_hbm.at[0], g, loc_sem.at[1]),
        pltpu.make_async_copy(k_hbm.at[0], kwin.at[BACK], loc_sem.at[2]),
        pltpu.make_async_copy(v_hbm.at[0], vwin.at[BACK], loc_sem.at[3]),
        pltpu.make_async_copy(
            x_hbm.at[0, :, pl.ds(pl.multiple_of(f * width, 128), width)], xg.at[f], loc_sem.at[4]
        ),
    ]
    for copy in local:
        copy.start()

    barrier = pltpu.get_barrier_semaphore()
    for d in range(1, BACK + 1):
        @pl.when(s >= d)
        def _():
            pl.semaphore_signal(
                barrier, inc=1, device_id={"seq": s - d, "fsdp": f}, device_id_type=MESH
            )

        @pl.when(s + d < n_s)
        def _():
            pl.semaphore_signal(
                barrier, inc=1, device_id={"seq": s + d, "fsdp": f}, device_id_type=MESH
            )
    for j in range(1, n_f):
        pl.semaphore_signal(
            barrier, inc=1, device_id={"seq": s, "fsdp": (f + j) % n_f}, device_id_type=MESH
        )

    def doc_of(block):
        end = jnp.int32(0)
        doc = jnp.int32(0)
        for i in range(doc_ref.shape[1]):
            end = end + doc_ref[0, i]
            doc = doc + jnp.where(block >= end, 1, 0)
        return doc

    mine = doc_of(s)
    for d in range(1, BACK + 1):
        seen = jnp.logical_and(doc_of(s - d) == mine, s >= d)
        level = jnp.where(seen, 0.0, -jnp.inf).astype(F32)
        bias[(BACK - d) * rows : (BACK - d + 1) * rows, :] = jnp.full(
            (rows, PAIR * rows), level, F32
        )
    key_at = lax.broadcasted_iota(jnp.int32, (rows, PAIR * rows), 0)
    query_at = lax.broadcasted_iota(jnp.int32, (rows, PAIR * rows), 1) % rows
    bias[BACK * rows :, :] = jnp.where(key_at <= query_at, 0.0, -jnp.inf).astype(F32)

    for d in range(1, BACK + 1):
        @pl.when(s < d)
        def _():
            kwin[BACK - d] = jnp.zeros((rows, kvw), BF16)
            vwin[BACK - d] = jnp.zeros((rows, kvw), BF16)

        @pl.when(s + d >= n_s)
        def _():
            dv_recv[d - 1] = jnp.zeros((rows, kvw), BF16)
            dk_recv[d - 1] = jnp.zeros((rows, kvw), BF16)

    @pl.when(z == 0)
    def _():
        left_recv[...] = jnp.zeros_like(left_recv)

    @pl.when(z == depth - 1)
    def _():
        right_recv[...] = jnp.zeros_like(right_recv)

    one = lambda c: jnp.where(c, 1, 0)
    pl.semaphore_wait(
        barrier, n_f - 1 + one(s >= 1) + one(s >= 2) + one(s + 1 < n_s) + one(s + 2 < n_s)
    )

    def group_cols(i):
        return pl.ds(pl.multiple_of(i * HEAD_SIZE, HEAD_SIZE), HEAD_SIZE)

    def k_copy(d, i):
        return remote(
            k_hbm.at[0, :, group_cols(i)], kwin.at[BACK - d, :, group_cols(i)],
            k_ss.at[d - 1, i], k_rs.at[d - 1, i], s + d, f,
        )

    def v_copy(d):
        return remote(
            v_hbm.at[0], vwin.at[BACK - d], v_ss.at[d - 1], v_rs.at[d - 1], s + d, f
        )

    def x_copy(j):
        to = (f + j) % n_f
        return remote(
            x_hbm.at[0, :, pl.ds(pl.multiple_of(to * width, 128), width)], xg.at[f],
            x_ss.at[j], x_rs.at[j], s, to,
        )

    for i in range(groups):
        for d in range(1, BACK + 1):
            @pl.when(s + d < n_s)
            def _():
                k_copy(d, i).start()
    for d in range(1, BACK + 1):
        @pl.when(s + d < n_s)
        def _():
            v_copy(d).start()
    for j in range(1, n_f):
        x_copy(j).start()

    for copy in local[:3]:
        copy.wait()

    def back_copy(send, recv, ss, rs, d, i):
        return remote(
            send.at[d - 1, :, group_cols(i)], recv.at[d - 1, :, group_cols(i)],
            ss.at[d - 1, i], rs.at[d - 1, i], s - d, f,
        )

    def pair_of(ref, i, j):
        first = (i * heads + j * PAIR) * HEAD_SIZE
        return jnp.concatenate(
            [
                ref[:, pl.ds(pl.multiple_of(first + n * HEAD_SIZE, HEAD_SIZE), HEAD_SIZE)]
                for n in range(PAIR)
            ],
            axis=0,
        )

    def give_back(total, own, send, recv, ss, rs, i):
        own[:, group_cols(i)] = total[BACK * rows :]
        for d in range(1, BACK + 1):
            send[d - 1, :, group_cols(i)] = total[(BACK - d) * rows : (BACK - d + 1) * rows].astype(
                BF16
            )

            @pl.when(s >= d)
            def _():
                back_copy(send, recv, ss, rs, d, i).start()

    def first_pass(i, carry):
        for d in range(1, BACK + 1):
            @pl.when(s >= d)
            def _():
                k_copy(d, i).wait_recv()
        k_group = kwin[:, :, group_cols(i)].reshape(keys, HEAD_SIZE)
        total = jnp.zeros((keys, HEAD_SIZE), F32)
        for j in range(heads // PAIR):
            scores = matmul(k_group, pair_of(q, i, j), 1, 1)
            scores = scores * (scale * math.log2(math.e)) + bias[...]
            exps = jnp.exp2(scores - jnp.max(scores, axis=0, keepdims=True))
            p = exps * (1.0 / jnp.sum(exps, axis=0, keepdims=True))
            probs[i, j] = p
            total = total + matmul(p.astype(BF16), pair_of(g, i, j), 1, 0)
        give_back(total, dv_own, dv_send, dv_recv, dv_ss, dv_rs, i)
        return carry

    lax.fori_loop(0, groups, first_pass, 0)

    local[3].wait()
    for d in range(1, BACK + 1):
        @pl.when(s >= d)
        def _():
            v_copy(d).wait_recv()

    def second_pass(i, carry):
        k_group = kwin[:, :, group_cols(i)].reshape(keys, HEAD_SIZE)
        v_group = vwin[:, :, group_cols(i)].reshape(keys, HEAD_SIZE)
        k_turned = k_group.T
        total = jnp.zeros((keys, HEAD_SIZE), F32)
        for j in range(heads // PAIR):
            p = probs[i, j]
            d_probs = matmul(v_group, pair_of(g, i, j), 1, 1)
            deltas = jnp.sum(p * d_probs, axis=0, keepdims=True)
            d_scores = (p * (d_probs - deltas)).astype(BF16)
            total = total + matmul(d_scores, pair_of(q, i, j), 1, 0)
            turned = (matmul(k_turned, d_scores, 1, 0) * scale).T.astype(BF16)
            first = (i * heads + j * PAIR) * HEAD_SIZE
            for n in range(PAIR):
                cols = pl.ds(pl.multiple_of(first + n * HEAD_SIZE, HEAD_SIZE), HEAD_SIZE)
                dq[:, cols] = turned[n * rows : (n + 1) * rows]
        give_back(total * scale, dk_own, dk_send, dk_recv, dk_ss, dk_rs, i)
        return carry

    def vg_copy(h, j):
        cols = pl.ds(h * half_cols, half_cols)
        return remote(
            vgb.at[f, :, cols], vgb.at[f, :, cols], vg_ss.at[h, j], vg_rs.at[h, j],
            s, (f + j) % n_f,
        )

    per_half = groups // HALVES

    def collect(own, recv, send, ss, rs, lo, count):
        for i in range(lo, lo + count):
            for d in range(1, BACK + 1):
                @pl.when(s + d < n_s)
                def _():
                    back_copy(send, recv, ss, rs, d, i).wait_recv()
        cols = slice(lo * HEAD_SIZE, (lo + count) * HEAD_SIZE)
        total = own[:, cols]
        for d in range(1, BACK + 1):
            total = total + recv[d - 1, :, cols].astype(F32)
        return total.astype(BF16)

    def value_half(h):
        cols = slice(h * half_cols, (h + 1) * half_cols)
        vgb[f, :, cols] = collect(dv_own, dv_recv, dv_send, dv_ss, dv_rs, h * per_half, per_half)
        for j in range(1, n_f):
            vg_copy(h, j).start()

    def pair_copy(h):
        return remote(
            pair_send.at[h], pair_recv.at[h], p_ss.at[h], p_rs.at[h], sibling, f
        )

    def weight_half(h):
        for j in range(1, n_f):
            vg_copy(h, j).wait_recv()
        values = vgb[:, :, h * half_cols : (h + 1) * half_cols].reshape(n_f * rows, half_cols)

        def part(which):
            lhs = xg[:, :, pl.ds(pl.multiple_of(which * half_rows, half_rows), half_rows)]
            return matmul(lhs.reshape(n_f * rows, half_rows), values, 0, 0)

        pair_send[h] = part(1 - core).astype(BF16)
        pair_copy(h).start()
        w_own[h] = part(core)

    lax.fori_loop(0, 1, second_pass, 0)
    value_half(0)
    lax.fori_loop(1, 2, second_pass, 0)
    value_half(1)
    lax.fori_loop(2, groups, second_pass, 0)
    dq_copy = pltpu.make_async_copy(dq, dq_out.at[0], out_sem.at[0])
    dq_copy.start()
    vg_save = pltpu.make_async_copy(vgb.at[f], vg_out.at[0], out_sem.at[1])
    vg_save.start()
    local[4].wait()
    for j in range(1, n_f):
        x_copy(j).wait_recv()
    for h in range(HALVES):
        weight_half(h)

    def right_copy(c):
        return remote(right_send.at[c], left_recv.at[c], r_ss.at[c], r_rs.at[c], s + 2, f)

    def left_copy(c):
        return remote(left_send.at[c], right_recv.at[c], l_ss.at[c], l_rs.at[c], s - 2, f)

    def place(c, side):
        at = side * half_rows + (c % SUB) * sub_rows
        return wfin.at[
            pl.ds(pl.multiple_of(at, sub_rows), sub_rows),
            pl.ds(pl.multiple_of((c // SUB) * half_cols, half_cols), half_cols),
        ]

    def final_copy(c):
        return remote(place(c, core), place(c, core), f_ss.at[c], f_rs.at[c], sibling, f)

    def own_chunk(c):
        return w_own[c // SUB, pl.ds(pl.multiple_of((c % SUB) * sub_rows, sub_rows), sub_rows), :]

    token_count = n_f * n_s * rows

    def step(t, carry):
        to_right = t - SLACK * z
        to_left = t - SLACK * (depth - 1 - z)
        done = t - SLACK * jnp.maximum(z, depth - 1 - z)

        def inside(c):
            return jnp.logical_and(c >= 0, c < chunks)

        @pl.when(jnp.logical_and(inside(to_right), z > 0))
        def _():
            right_copy(to_right).wait_recv()

        @pl.when(jnp.logical_and(inside(to_right), z < depth - 1))
        def _():
            right_send[to_right] = (own_chunk(to_right) + left_recv[to_right].astype(F32)).astype(
                BF16
            )
            right_copy(to_right).start()

        @pl.when(jnp.logical_and(inside(to_left), z < depth - 1))
        def _():
            left_copy(to_left).wait_recv()

        @pl.when(jnp.logical_and(inside(to_left), z > 0))
        def _():
            left_send[to_left] = (own_chunk(to_left) + right_recv[to_left].astype(F32)).astype(BF16)
            left_copy(to_left).start()

        @pl.when(inside(done))
        def _():
            total = own_chunk(done) + left_recv[done].astype(F32) + right_recv[done].astype(F32)
            place(done, core)[...] = (total * (1.0 / math.sqrt(token_count))).astype(BF16)
            final_copy(done).start()

        return carry

    for h in range(HALVES):
        pair_copy(h).wait_recv()
        w_own[h] = w_own[h] + pair_recv[h].astype(F32)
        last = (h + 1) * SUB if h < HALVES - 1 else chunks + SLACK * (depth - 1)
        lax.fori_loop(h * SUB, last, step, 0)

    dkb[...] = collect(dk_own, dk_recv, dk_send, dk_ss, dk_rs, 0, groups)
    dk_save = pltpu.make_async_copy(dkb, dk_out.at[0], out_sem.at[2])
    dk_save.start()

    def settle(c, carry):
        other = remote(place(c, 1 - core), place(c, 1 - core), f_ss.at[c], f_rs.at[c], sibling, f)
        other.wait_recv()
        final_copy(c).wait_send()

        @pl.when(z < depth - 1)
        def _():
            right_copy(c).wait_send()

        @pl.when(z > 0)
        def _():
            left_copy(c).wait_send()

        return carry

    lax.fori_loop(0, chunks, settle, 0)
    w_save = pltpu.make_async_copy(wfin, w_out, out_sem.at[3])
    w_save.start()
    for d in range(1, BACK + 1):
        @pl.when(s + d < n_s)
        def _():
            v_copy(d).wait_send()
            for i in range(groups):
                k_copy(d, i).wait_send()

        @pl.when(s >= d)
        def _():
            for i in range(groups):
                back_copy(dv_send, dv_recv, dv_ss, dv_rs, d, i).wait_send()
                back_copy(dk_send, dk_recv, dk_ss, dk_rs, d, i).wait_send()
    for j in range(1, n_f):
        x_copy(j).wait_send()
        for h in range(HALVES):
            vg_copy(h, j).wait_send()
    for h in range(HALVES):
        pair_copy(h).wait_send()
    dq_copy.wait()
    vg_save.wait()
    dk_save.wait()
    w_save.wait()


def settle_outputs(*refs):
    sources, outs, held = refs[:4], refs[4:8], refs[8:12]
    in_sem, out_sem = refs[12:]
    loads, saves = [], []
    for i in range(4):
        loads.append(pltpu.make_async_copy(sources[i], held[i], in_sem.at[i]))
        saves.append(pltpu.make_async_copy(held[i], outs[i], out_sem.at[i]))
    for load in loads:
        load.start()
    for load, save in zip(loads, saves):
        load.wait()
        save.start()
    for save in saves:
        save.wait()


def shards(n_s, n_f, layer_inputs, queries, key_states, value_states, output_gradient, doc_blocks):
    rows = queries.shape[1]
    kvw = key_states.shape[2]
    groups = kvw // HEAD_SIZE
    heads = queries.shape[2] // kvw
    width = layer_inputs.shape[2] // n_f
    chunks = HALVES * SUB
    half_cols = kvw // HALVES
    half_rows = width // 2
    sub_rows = half_rows // SUB
    keys = (BACK + 1) * rows
    V = pltpu.VMEM
    D = pltpu.SemaphoreType.DMA
    scratch = [
        V((rows, queries.shape[2]), BF16),
        V((rows, queries.shape[2]), BF16),
        V((BACK + 1, rows, kvw), BF16),
        V((BACK + 1, rows, kvw), BF16),
        V((n_f, rows, width), BF16),
        V((groups, heads // PAIR, keys, PAIR * rows), F32),
        V((keys, PAIR * rows), F32),
        V((rows, queries.shape[2]), BF16),
        V((rows, kvw), F32),
        V((BACK, rows, kvw), BF16),
        V((BACK, rows, kvw), BF16),
        V((rows, kvw), F32),
        V((BACK, rows, kvw), BF16),
        V((BACK, rows, kvw), BF16),
        V((rows, kvw), BF16),
        V((n_f, rows, kvw), BF16),
        V((HALVES, half_rows, half_cols), F32),
        V((HALVES, half_rows, half_cols), BF16),
        V((HALVES, half_rows, half_cols), BF16),
        V((chunks, sub_rows, half_cols), BF16),
        V((chunks, sub_rows, half_cols), BF16),
        V((chunks, sub_rows, half_cols), BF16),
        V((chunks, sub_rows, half_cols), BF16),
        V((width, kvw), BF16),
        D((5,)), D((4,)),
        D((BACK, groups)), D((BACK, groups)), D((BACK,)), D((BACK,)), D((n_f,)), D((n_f,)),
        D((BACK, groups)), D((BACK, groups)), D((BACK, groups)), D((BACK, groups)),
        D((HALVES, n_f)), D((HALVES, n_f)), D((HALVES,)), D((HALVES,)),
        D((chunks,)), D((chunks,)), D((chunks,)), D((chunks,)), D((chunks,)), D((chunks,)),
    ]
    anywhere = pl.BlockSpec(memory_space=pl.ANY)
    out_shape = [
        jax.ShapeDtypeStruct(queries.shape, BF16),
        jax.ShapeDtypeStruct(key_states.shape, BF16),
        jax.ShapeDtypeStruct(key_states.shape, BF16),
        jax.ShapeDtypeStruct((width, kvw), BF16),
    ]
    made = (
        pl.pallas_call(
            functools.partial(kernel, n_s, n_f, groups, heads),
            out_shape=out_shape,
            in_specs=[pl.BlockSpec(memory_space=pltpu.SMEM)] + [anywhere] * 5,
            out_specs=[anywhere] * 4,
            scratch_shapes=scratch,
            compiler_params=pltpu.CompilerParams(collective_id=0, has_side_effects=True),
        )(doc_blocks, layer_inputs, queries, key_states, value_states, output_gradient)
    )
    return tuple(
        pl.pallas_call(
            settle_outputs,
            out_shape=out_shape,
            in_specs=[anywhere] * 4,
            out_specs=[anywhere] * 4,
            scratch_shapes=[V(o.shape, BF16) for o in out_shape] + [D((4,)), D((4,))],
        )(*made)
    )


def solution(mesh):
    sizes = dict(mesh.shape)
    return jax.shard_map(
        functools.partial(shards, sizes["seq"], sizes["fsdp"]),
        mesh=mesh,
        in_specs=(P("fsdp", "seq", None),) * 5 + (P("fsdp", None),),
        out_specs=(P("fsdp", "seq", None),) * 3 + (P("fsdp", None),),
        check_vma=False,
    )
```
